768 devices in a mesh: mem: 6 (over z_hi, core), lat: 128 (over y, x, z_lo).
Axes of the slice: x: 4, y: 8, z: 12 (z_hi: 3, z_lo: 4; z = z_hi * 4 + z_lo), core: 2. Of those that a mesh axis runs over, the one named last changes fastest.
Arguments:
- perturbations: bfloat16 [96, 2, 12, 512, 1440], P('mem', None, None, 'lat'), may hold values from -1 to 1
- gradient_held: float32 [2, 12, 512, 1440], P(None, 'mem', 'lat'), may hold values from -6 to 6
- block_owner: int32 [12], replicated, may hold values from 0 to 11, each once
Outputs:
- increment_held: float32 [2, 12, 512, 1440], P(None, 'mem', 'lat')
The draws below stay inside these ranges and needn't reach their ends.
Inputs may be any that keep to these rules, and one draw needn't show every extreme that they name: `block_owner`: each value appears exactly once.
All inputs are finite; a program needn't handle non-finite values.
Results may differ from the reference program's by a relative error of at most 0.0022.
Values may be sent and summed in bfloat16 or wider, within the bound.
No kernel may reach another device: no remote copies, remote signals or barrier semaphores. Data moves between devices by JAX's collectives and lax.ppermute only.
A program may use at most 128 MiB of HBM per device.

```python
import math
import jax
import jax.numpy as jnp
from jax import lax

LON = 1440
SLOTS = 2
MEMBERS = 96
LEV = 12
LAT = 512


def draw_perturbations(key, part):
    subkeys = jax.random.split(key, 1)
    full_shape = (MEMBERS, SLOTS, LEV, LAT, LON)
    spread = 1.0 / math.sqrt(MEMBERS)
    white_noise = jax.random.normal(subkeys[0], full_shape, jnp.float32)
    values = spread * white_noise
    return jnp.clip(values, -1.0, 1.0).astype(jnp.bfloat16)


def draw_gradient_held(key, part):
    subkeys = jax.random.split(key, 1)
    full_shape = (SLOTS, LEV, LAT, LON)
    white_noise = jax.random.normal(subkeys[0], full_shape, jnp.float32)
    values = white_noise
    return jnp.clip(values, -6.0, 6.0).astype(jnp.float32)


def setup_inputs(seed: int = 0) -> dict:
    streams_of = jax.random.split(jax.random.key(seed), 4)
    perturbations = draw_perturbations(jax.random.fold_in(streams_of[3], 71), 0)
    gradient_held = draw_gradient_held(jax.random.fold_in(streams_of[3], 71), 0)
    block_owner = jax.random.permutation(streams_of[2], LEV).astype(jnp.int32)
    return dict(perturbations=perturbations, gradient_held=gradient_held, block_owner=block_owner)


def weights_for(spread_cells):
    return [math.exp(-(offset * offset) / (2.0 * spread_cells * spread_cells)) for offset in range(-4, 5)]


def smooth_periodic(source, along_dim, weights):
    summed = jnp.zeros_like(source)
    for offset in range(-4, 5):
        summed = summed + weights[offset + 4] * jnp.roll(source, -offset, axis=along_dim)
    return summed


def smooth_bounded(source, along_dim, weights):
    length = source.shape[along_dim]
    widths = [(0, 0)] * source.ndim
    widths[along_dim] = (4, 4)
    padded = jnp.pad(source, widths)
    summed = jnp.zeros_like(source)
    for offset in range(-4, 5):
        summed = summed + weights[offset + 4] * lax.slice_in_dim(padded, 4 + offset, 4 + offset + length, axis=along_dim)
    return summed


def reference(perturbations, gradient_held, block_owner):
    places = jnp.arange(LEV, dtype=jnp.int32)
    owners = block_owner.astype(jnp.int32)
    inverse = jnp.sum(jnp.where(owners[None, :] == places[:, None], places[None, :], 0), axis=1).astype(jnp.int32)
    gradient = jnp.take(gradient_held, inverse, axis=1)
    lon_weights = weights_for(3.0)
    lev_weights = weights_for(2.0)
    lat_weights = weights_for(2.5)

    def member_step(summed, member):
        widened = member.astype(jnp.float32)
        control = jnp.sum(widened * gradient, axis=0).astype(jnp.bfloat16)
        control = lax.optimization_barrier(control).astype(jnp.float32)
        smoothed = smooth_periodic(control, 2, lon_weights)
        smoothed = smooth_bounded(smoothed, 0, lev_weights)
        smoothed = smooth_bounded(smoothed, 1, lat_weights)
        return summed + widened * smoothed[None], None

    start = jnp.zeros((SLOTS, LEV, LAT, LON), jnp.float32)
    increment, unused = lax.scan(member_step, start, perturbations)
    return jnp.take(increment, owners, axis=1)
```

```python
import functools
import math

import jax
import jax.numpy as jnp
from jax import lax
from jax.experimental import pallas as pl
from jax.experimental.pallas import tpu as pltpu
from jax.sharding import PartitionSpec as P

LANES = 128
VMEM_LIMIT = 24 * 1024 * 1024
COST = pl.CostEstimate(flops=1000, bytes_accessed=1000, transcendentals=0)


def weights_for(spread_cells):
    return [
        math.exp(-(offset * offset) / (2.0 * spread_cells * spread_cells))
        for offset in range(-4, 5)
    ]


LON_W = weights_for(3.0)
LEV_W = weights_for(2.0)
LAT_W = weights_for(2.5)


def prepare_kernel(levels_ref, pert_ref, grad_ref, *refs):
    turned_ref, packed_ref = refs[-2:]
    slots, rows, lon = grad_ref.shape[1], grad_ref.shape[3], grad_ref.shape[4]
    full = lon // LANES
    for slot in range(slots):
        turned = jnp.transpose(pert_ref[:, slot, 0].astype(jnp.float32), (1, 0, 2))
        turned_ref[0, :, slot] = turned.astype(jnp.bfloat16)
    tails = []
    for row in range(rows):
        for tile in range(full + 1):
            lanes = slice(tile * LANES, min((tile + 1) * LANES, lon))
            value = None
            for slot in range(slots):
                term = (
                    turned_ref[0, row, slot, :, lanes].astype(jnp.float32)
                    * grad_ref[0, slot, 0, row : row + 1, lanes]
                )
                value = term if value is None else value + term
            if tile < full:
                packed_ref[0, row * full + tile] = value.astype(jnp.bfloat16)
            else:
                tails.append(value)
    packed_ref[0, rows * full] = jnp.concatenate(tails, axis=1).astype(jnp.bfloat16)


def prepare(first, size, levels, perturbations, gradient, turned=None, limit=VMEM_LIMIT):
    members, slots, count, rows, lon = perturbations.shape
    entries = rows * (lon // LANES) + 1
    inputs = [perturbations, gradient]
    in_specs = [
        pl.BlockSpec(
            (members, slots, 1, rows, lon), lambda i, lev: (0, 0, lev[i], 0, 0)
        ),
        pl.BlockSpec((1, slots, 1, rows, lon), lambda i, lev: (i // 2, 0, i % 2, 0, 0)),
    ]
    aliases = {}
    if turned is not None:
        inputs.append(turned)
        in_specs.append(pl.BlockSpec(memory_space=pl.ANY))
        aliases = {3: 0}
    return pl.pallas_call(
        prepare_kernel,
        out_shape=(
            jax.ShapeDtypeStruct((count, rows, slots, members, lon), jnp.bfloat16),
            jax.ShapeDtypeStruct((size, entries, members, LANES), jnp.bfloat16),
        ),
        grid_spec=pltpu.PrefetchScalarGridSpec(
            num_scalar_prefetch=1,
            grid=(size,),
            in_specs=in_specs,
            out_specs=(
                pl.BlockSpec(
                    (1, rows, slots, members, lon),
                    lambda i, lev: (2 * first + i, 0, 0, 0, 0),
                ),
                pl.BlockSpec((1, entries, members, LANES), lambda i, lev: (i, 0, 0, 0)),
            ),
        ),
        input_output_aliases=aliases,
        name="prepare",
        cost_estimate=COST,
        compiler_params=pltpu.CompilerParams(vmem_limit_bytes=limit),
    )(levels, *inputs)


def smooth_level(refs, out_ref, level, wide_ref, rows, lon):
    full, rest = lon // LANES, lon % LANES
    members = refs[0].shape[2]
    for tile in range(full + 1):
        if tile < full:
            source = [
                ref[0, row * full + tile].astype(jnp.float32) for ref in refs for row in range(rows)
            ]
        else:
            tails = [ref[0, rows * full].astype(jnp.float32) for ref in refs]
            source = [
                tail if row == 0 else pltpu.roll(tail, LANES - row * rest, 1)
                for tail in tails
                for row in range(rows)
            ]
        for row in range(rows):
            total = LAT_W[4] * source[row + 4]
            for step in range(1, 5):
                total = total + LAT_W[4 + step] * (source[row + 4 - step] + source[row + 4 + step])
            wide_ref[row, :, tile * LANES : (tile + 1) * LANES] = total
    half = 8
    lane = lax.broadcasted_iota(jnp.int32, (half, LANES), 1)
    for row in range(rows):
        for part in range(members // half):
            some = slice(part * half, (part + 1) * half)
            tiles = [
                wide_ref[row, some, tile * LANES : (tile + 1) * LANES] for tile in range(full + 1)
            ]
            before = pltpu.roll(tiles[full], LANES - rest, 1)
            tiles[full] = jnp.where(lane < rest, tiles[full], pltpu.roll(tiles[0], rest, 1))
            tiles = [before] + tiles
            totals = [LON_W[4] * tile for tile in tiles[1:]]
            for step in range(1, 5):
                right = [pltpu.roll(tile, step, 1) for tile in tiles]
                left = [pltpu.roll(tile, LANES - step, 1) for tile in tiles[1:]]
                left.append(left[-1])
                for tile in range(full + 1):
                    both = jnp.where(lane < step, right[tile], right[tile + 1]) + jnp.where(
                        lane < LANES - step, left[tile], left[tile + 1]
                    )
                    totals[tile] = totals[tile] + LON_W[4 + step] * both
            for tile in range(full + 1):
                out_ref[level, row, some, tile * LANES : (tile + 1) * LANES] = totals[tile]


def sums_of(arrays, sub):
    for width in (1, 2, 4):
        low = (sub & width) == 0
        arrays = [
            jnp.where(low, even, odd) + pltpu.roll(jnp.where(low, odd, even), width, 0)
            for even, odd in zip(arrays[::2], arrays[1::2])
        ]
    return arrays[0]


def collect_pair(pair, first, fields_ref, weight_ref, pert_ref, before_ref, out_ref, lon):
    size, rows, members, _ = fields_ref.shape
    full = lon // LANES
    slots = out_ref.shape[0]
    weights = [
        [weight_ref[2 * pair + i, 2 * first + source] for source in range(size)]
        for i in range(2)
    ]
    for tile in range(full + 1):
        lanes = slice(tile * LANES, min((tile + 1) * LANES, lon))
        across = min((tile + 1) * LANES, lon) - tile * LANES
        sub = lax.broadcasted_iota(jnp.int32, (8, across), 0)
        products = [[[None] * rows for _ in range(slots)] for _ in range(2)]
        for row in range(rows):
            values = [fields_ref[source, row, :, lanes] for source in range(size)]
            for i in range(2):
                total = weights[i][0] * values[0]
                for source in range(1, size):
                    total = total + weights[i][source] * values[source]
                for slot in range(slots):
                    product = total * pert_ref[i, row, slot, :, lanes].astype(jnp.float32)
                    product = product.reshape(members // 8, 8, across)
                    part = product[0]
                    for other in range(1, members // 8):
                        part = part + product[other]
                    products[i][slot][row] = part
        for i in range(2):
            value = sums_of(products[i][0] + products[i][1], sub)
            for slot in range(slots):
                piece = value[slot * rows : (slot + 1) * rows]
                if before_ref is not None:
                    piece = piece + before_ref[slot, i, :, lanes]
                out_ref[slot, i, :, lanes] = piece


def collect_kernel(weight_ref, low_ref, own_ref, high_ref, pert_ref, *refs, first, lon):
    theirs_ref, ours_ref, fields_ref, wide_ref = refs[-4:]
    theirs_before, ours_before = refs[:2] if len(refs) > 4 else (None, None)
    size, rows = fields_ref.shape[:2]
    step = pl.program_id(0)
    half = (pl.num_programs(0) - size) // 2

    @pl.when(step < size)
    def _():
        smooth_level((low_ref, own_ref, high_ref), fields_ref, step, wide_ref, rows, lon)

    @pl.when((step >= size) & (step < size + half))
    def _():
        pair = step - size + half
        collect_pair(
            pair, first, fields_ref, weight_ref, pert_ref, theirs_before, theirs_ref, lon
        )

    @pl.when(step >= size + half)
    def _():
        pair = step - size - half
        collect_pair(pair, first, fields_ref, weight_ref, pert_ref, ours_before, ours_ref, lon)


def collect(first, weights, low, own, high, turned, before):
    count, rows, slots, members, lon = turned.shape
    size, entries = own.shape[:2]
    pairs = count // 2
    half = pairs // 2
    width = (lon // LANES + 1) * LANES
    level = pl.BlockSpec(
        (1, entries, members, LANES), lambda i, w: (jnp.minimum(i, size - 1), 0, 0, 0)
    )
    theirs = pl.BlockSpec(
        (slots, 2, rows, lon), lambda i, w: (0, jnp.clip(i - size, 0, half - 1), 0, 0)
    )
    ours = pl.BlockSpec(
        (slots, 2, rows, lon), lambda i, w: (0, jnp.clip(i - size - half, 0, half - 1), 0, 0)
    )
    pert = pl.BlockSpec(
        (2, rows, slots, members, lon),
        lambda i, w: ((jnp.maximum(i - size, 0) + half) % pairs, 0, 0, 0, 0),
    )
    result = jax.ShapeDtypeStruct((slots, count // 2, rows, lon), jnp.float32)
    return pl.pallas_call(
        functools.partial(collect_kernel, first=first, lon=lon),
        out_shape=(result, result),
        grid_spec=pltpu.PrefetchScalarGridSpec(
            num_scalar_prefetch=1,
            grid=(size + pairs,),
            in_specs=[level] * 3 + [pert] + ([] if before is None else [theirs, ours]),
            out_specs=(theirs, ours),
            scratch_shapes=[
                pltpu.VMEM((size, rows, members, width), jnp.float32),
                pltpu.VMEM((rows, members, width), jnp.float32),
            ],
        ),
        name="collect",
        cost_estimate=COST,
        compiler_params=pltpu.CompilerParams(vmem_limit_bytes=VMEM_LIMIT),
    )(weights, low, own, high, turned, *(() if before is None else before))


def local(perturbations, gradient_held, block_owner):
    members, slots, levels, rows, lon = perturbations.shape
    across = lax.axis_size("mem") // 2
    place = lax.axis_index("mem")
    high, core = place // 2, place % 2

    swap = [(2 * z + c, 2 * z + 1 - c) for z in range(across) for c in range(2)]
    down = [(2 * ((z + 1) % across) + c, 2 * z + c) for z in range(across) for c in range(2)]
    up = [(2 * z + c, 2 * ((z + 1) % across) + c) for z in range(across) for c in range(2)]
    count = lax.axis_size("lat")
    forward = [(i, i + 1) for i in range(count - 1)]
    backward = [(i + 1, i) for i in range(count - 1)]

    index = jnp.arange(levels, dtype=jnp.int32)
    pair = index // 2
    shift = jnp.where(pair % 3 == 0, 0, jnp.where(pair % 3 == 1, 1, across - 1))
    flip = jnp.where(pair >= 3, 1 - core, core)
    positions = 2 * (2 * ((high + shift) % across) + flip) + index % 2
    order = jnp.sum(
        jnp.where(
            positions[:, None] == index[None, :], block_owner.astype(jnp.int32)[None, :], 0
        ),
        axis=1,
    ).astype(jnp.int32)
    apart = jnp.abs(order[:, None] - order[None, :])
    weights = jnp.zeros((levels, levels), jnp.float32)
    for step in range(5):
        weights = jnp.where(apart == step, LEV_W[4 + step], weights)

    def halos(control, after=None):
        lower, upper = control, control
        if after is not None:
            lower, _ = lax.optimization_barrier((control, after[0]))
            upper, _ = lax.optimization_barrier((control, after[1]))
        return lax.ppermute(lower, "lat", forward), lax.ppermute(upper, "lat", backward)

    held = lax.dynamic_slice_in_dim(block_owner.astype(jnp.int32), 2 * place, 2)
    turned, own = prepare(
        0, 2, held, perturbations, gradient_held[None], limit=57 * 1024 * 1024
    )
    own_low, own_high = halos(own)
    near = [
        lax.ppermute(gradient_held, "mem", down),
        lax.ppermute(gradient_held, "mem", up),
        lax.ppermute(gradient_held, "mem", swap),
    ]
    near = jnp.stack(near)
    far = lax.ppermute(near, "mem", swap)
    turned, mid = prepare(1, 6, order[2:8], perturbations, near, turned)
    mid_low, mid_high = halos(mid, (own_low, own_high))
    turned, last = prepare(4, 4, order[8:], perturbations, far, turned)
    last_low, last_high = halos(last)

    sums = collect(0, weights, own_low, own, own_high, turned, None)
    sums = collect(1, weights, mid_low, mid, mid_high, turned, sums)
    theirs, ours = collect(4, weights, last_low, last, last_high, turned, sums)
    kept = ours + lax.ppermute(theirs, "mem", swap)
    from_below = lax.ppermute(kept[:, 2:4].astype(jnp.bfloat16), "mem", up)
    from_above = lax.ppermute(kept[:, 4:6].astype(jnp.bfloat16), "mem", down)
    return kept[:, :2] + from_below.astype(jnp.float32) + from_above.astype(jnp.float32)


def solution(mesh):
    placed = (P("mem", None, None, "lat", None), P(None, "mem", "lat", None), P())
    return jax.shard_map(
        local, mesh=mesh, in_specs=placed, out_specs=P(None, "mem", "lat", None), check_vma=False
    )
```

```python
import functools
import math

import jax
import jax.numpy as jnp
from jax import lax
from jax.experimental import pallas as pl
from jax.experimental.pallas import tpu as pltpu
from jax.sharding import PartitionSpec as P

LANES = 128
VMEM_LIMIT = 24 * 1024 * 1024
COST = pl.CostEstimate(flops=1000, bytes_accessed=1000, transcendentals=0)


def weights_for(spread_cells):
    return [
        math.exp(-(offset * offset) / (2.0 * spread_cells * spread_cells))
        for offset in range(-4, 5)
    ]


LON_W = weights_for(3.0)
LEV_W = weights_for(2.0)
LAT_W = weights_for(2.5)


def prepare_kernel(levels_ref, base_ref, pert_ref, grad_ref, *refs):
    turned_ref, packed_ref = refs[-2:]
    slots, rows, lon = grad_ref.shape[1], grad_ref.shape[3], grad_ref.shape[4]
    full = lon // LANES
    for slot in range(slots):
        turned = jnp.transpose(pert_ref[:, slot, 0].astype(jnp.float32), (1, 0, 2))
        turned_ref[0, :, slot] = turned.astype(jnp.bfloat16)
    tails = []
    for row in range(rows):
        for tile in range(full + 1):
            lanes = slice(tile * LANES, min((tile + 1) * LANES, lon))
            value = None
            for slot in range(slots):
                term = (
                    turned_ref[0, row, slot, :, lanes].astype(jnp.float32)
                    * grad_ref[0, slot, 0, row : row + 1, lanes]
                )
                value = term if value is None else value + term
            if tile < full:
                packed_ref[0, row * full + tile] = value.astype(jnp.bfloat16)
            else:
                tails.append(value)
    packed_ref[0, rows * full] = jnp.concatenate(tails, axis=1).astype(jnp.bfloat16)


def prepare(
    first, size, levels, base, perturbations, gradient, skip=0, turned=None
):
    members, slots, count, rows, lon = perturbations.shape
    entries = rows * (lon // LANES) + 1
    inputs = [perturbations, gradient]
    in_specs = [
        pl.BlockSpec(
            (members, slots, 1, rows, lon), lambda i, lev, b: (0, 0, lev[b[0] + i], 0, 0)
        ),
        pl.BlockSpec(
            (1, slots, 1, rows, lon),
            lambda i, lev, b: ((i + skip) // 2, 0, (i + skip) % 2, 0, 0),
        ),
    ]
    aliases = {}
    if turned is not None:
        inputs.append(turned)
        in_specs.append(pl.BlockSpec(memory_space=pl.ANY))
        aliases = {4: 0}
    return pl.pallas_call(
        prepare_kernel,
        out_shape=(
            jax.ShapeDtypeStruct((count, rows, slots, members, lon), jnp.bfloat16),
            jax.ShapeDtypeStruct((size, entries, members, LANES), jnp.bfloat16),
        ),
        grid_spec=pltpu.PrefetchScalarGridSpec(
            num_scalar_prefetch=2,
            grid=(size,),
            in_specs=in_specs,
            out_specs=(
                pl.BlockSpec(
                    (1, rows, slots, members, lon),
                    lambda i, lev, b: (first + i, 0, 0, 0, 0),
                ),
                pl.BlockSpec((1, entries, members, LANES), lambda i, lev, b: (i, 0, 0, 0)),
            ),
        ),
        input_output_aliases=aliases,
        name="prepare",
        cost_estimate=COST,
        compiler_params=pltpu.CompilerParams(vmem_limit_bytes=57 * 1024 * 1024),
    )(levels, base, *inputs)


def smooth_level(refs, out_ref, level, wide_ref, rows, lon):
    full, rest = lon // LANES, lon % LANES
    members = refs[0].shape[2]
    for tile in range(full + 1):
        if tile < full:
            source = [
                ref[0, row * full + tile].astype(jnp.float32) for ref in refs for row in range(rows)
            ]
        else:
            tails = [ref[0, rows * full].astype(jnp.float32) for ref in refs]
            source = [
                tail if row == 0 else pltpu.roll(tail, LANES - row * rest, 1)
                for tail in tails
                for row in range(rows)
            ]
        for row in range(rows):
            total = LAT_W[4] * source[row + 4]
            for step in range(1, 5):
                total = total + LAT_W[4 + step] * (source[row + 4 - step] + source[row + 4 + step])
            wide_ref[row, :, tile * LANES : (tile + 1) * LANES] = total
    half = 8
    lane = lax.broadcasted_iota(jnp.int32, (half, LANES), 1)
    for row in range(rows):
        for part in range(members // half):
            some = slice(part * half, (part + 1) * half)
            tiles = [
                wide_ref[row, some, tile * LANES : (tile + 1) * LANES] for tile in range(full + 1)
            ]
            before = pltpu.roll(tiles[full], LANES - rest, 1)
            tiles[full] = jnp.where(lane < rest, tiles[full], pltpu.roll(tiles[0], rest, 1))
            tiles = [before] + tiles
            totals = [LON_W[4] * tile for tile in tiles[1:]]
            for step in range(1, 5):
                right = [pltpu.roll(tile, step, 1) for tile in tiles]
                left = [pltpu.roll(tile, LANES - step, 1) for tile in tiles[1:]]
                left.append(left[-1])
                for tile in range(full + 1):
                    both = jnp.where(lane < step, right[tile], right[tile + 1]) + jnp.where(
                        lane < LANES - step, left[tile], left[tile + 1]
                    )
                    totals[tile] = totals[tile] + LON_W[4 + step] * both
            for tile in range(full + 1):
                out_ref[level, row, some, tile * LANES : (tile + 1) * LANES] = totals[tile]


def sums_of(arrays, sub):
    for width in (1, 2, 4):
        low = (sub & width) == 0
        arrays = [
            jnp.where(low, even, odd) + pltpu.roll(jnp.where(low, odd, even), width, 0)
            for even, odd in zip(arrays[::2], arrays[1::2])
        ]
    return arrays[0]


def collect_pair(pair, first, fields_ref, weight_ref, pert_ref, before_ref, out_ref, lon):
    size, rows, members, _ = fields_ref.shape
    full = lon // LANES
    slots = out_ref.shape[0]
    weights = [
        [weight_ref[2 * pair + i, first + source] for source in range(size)]
        for i in range(2)
    ]
    for tile in range(full + 1):
        lanes = slice(tile * LANES, min((tile + 1) * LANES, lon))
        across = min((tile + 1) * LANES, lon) - tile * LANES
        sub = lax.broadcasted_iota(jnp.int32, (8, across), 0)
        products = [[[None] * rows for _ in range(slots)] for _ in range(2)]
        for row in range(rows):
            values = [fields_ref[source, row, :, lanes] for source in range(size)]
            for i in range(2):
                total = weights[i][0] * values[0]
                for source in range(1, size):
                    total = total + weights[i][source] * values[source]
                for slot in range(slots):
                    product = total * pert_ref[i, row, slot, :, lanes].astype(jnp.float32)
                    product = product.reshape(members // 8, 8, across)
                    part = product[0]
                    for other in range(1, members // 8):
                        part = part + product[other]
                    products[i][slot][row] = part
        for i in range(2):
            value = sums_of(products[i][0] + products[i][1], sub)
            for slot in range(slots):
                piece = value[slot * rows : (slot + 1) * rows]
                if before_ref is not None:
                    piece = piece + before_ref[slot, i, :, lanes]
                out_ref[slot, i, :, lanes] = piece


def collect_kernel(weight_ref, low_ref, own_ref, high_ref, pert_ref, *refs, first, lon):
    theirs_ref, ours_ref, fields_ref, wide_ref = refs[-4:]
    theirs_before, ours_before = refs[:2] if len(refs) > 4 else (None, None)
    size, rows = fields_ref.shape[:2]
    step = pl.program_id(0)
    half = (pl.num_programs(0) - size) // 2

    @pl.when(step < size)
    def _():
        smooth_level((low_ref, own_ref, high_ref), fields_ref, step, wide_ref, rows, lon)

    @pl.when((step >= size) & (step < size + half))
    def _():
        pair = step - size + half
        collect_pair(
            pair, first, fields_ref, weight_ref, pert_ref, theirs_before, theirs_ref, lon
        )

    @pl.when(step >= size + half)
    def _():
        pair = step - size - half
        collect_pair(pair, first, fields_ref, weight_ref, pert_ref, ours_before, ours_ref, lon)


def collect(first, weights, low, own, high, turned, before):
    count, rows, slots, members, lon = turned.shape
    size, entries = own.shape[:2]
    pairs = count // 2
    half = pairs // 2
    width = (lon // LANES + 1) * LANES
    level = pl.BlockSpec(
        (1, entries, members, LANES), lambda i, w: (jnp.minimum(i, size - 1), 0, 0, 0)
    )
    theirs = pl.BlockSpec(
        (slots, 2, rows, lon), lambda i, w: (0, jnp.clip(i - size, 0, half - 1), 0, 0)
    )
    ours = pl.BlockSpec(
        (slots, 2, rows, lon), lambda i, w: (0, jnp.clip(i - size - half, 0, half - 1), 0, 0)
    )
    pert = pl.BlockSpec(
        (2, rows, slots, members, lon),
        lambda i, w: ((jnp.maximum(i - size, 0) + half) % pairs, 0, 0, 0, 0),
    )
    result = jax.ShapeDtypeStruct((slots, count // 2, rows, lon), jnp.float32)
    return pl.pallas_call(
        functools.partial(collect_kernel, first=first, lon=lon),
        out_shape=(result, result),
        grid_spec=pltpu.PrefetchScalarGridSpec(
            num_scalar_prefetch=1,
            grid=(size + pairs,),
            in_specs=[level] * 3 + [pert] + ([] if before is None else [theirs, ours]),
            out_specs=(theirs, ours),
            scratch_shapes=[
                pltpu.VMEM((size, rows, members, width), jnp.float32),
                pltpu.VMEM((rows, members, width), jnp.float32),
            ],
        ),
        name="collect",
        cost_estimate=COST,
        compiler_params=pltpu.CompilerParams(vmem_limit_bytes=VMEM_LIMIT),
    )(weights, low, own, high, turned, *(() if before is None else before))


def local(perturbations, gradient_held, block_owner):
    members, slots, levels, rows, lon = perturbations.shape
    across = lax.axis_size("mem") // 2
    place = lax.axis_index("mem")
    high, core = place // 2, place % 2

    swap = [(2 * z + c, 2 * z + 1 - c) for z in range(across) for c in range(2)]
    down = [(2 * ((z + 1) % across) + c, 2 * z + c) for z in range(across) for c in range(2)]
    up = [(2 * z + c, 2 * ((z + 1) % across) + c) for z in range(across) for c in range(2)]
    count = lax.axis_size("lat")
    forward = [(i, i + 1) for i in range(count - 1)]
    backward = [(i + 1, i) for i in range(count - 1)]

    index = jnp.arange(levels, dtype=jnp.int32)
    pair = index // 2
    shift = jnp.where(pair % 3 == 0, 0, jnp.where(pair % 3 == 1, 1, across - 1))
    flip = jnp.where(pair >= 3, 1 - core, core)
    positions = 2 * (2 * ((high + shift) % across) + flip) + index % 2
    order = jnp.sum(
        jnp.where(
            positions[:, None] == index[None, :], block_owner.astype(jnp.int32)[None, :], 0
        ),
        axis=1,
    ).astype(jnp.int32)
    apart = jnp.abs(order[:, None] - order[None, :])
    weights = jnp.zeros((levels, levels), jnp.float32)
    for step in range(5):
        weights = jnp.where(apart == step, LEV_W[4 + step], weights)

    def halos(control):
        return lax.ppermute(control, "lat", forward), lax.ppermute(control, "lat", backward)

    turned, own = prepare(
        0,
        2,
        block_owner.astype(jnp.int32),
        (2 * place).astype(jnp.int32).reshape(1),
        perturbations,
        gradient_held[None],
    )
    own_low, own_high = halos(own)
    gradient_here, _ = lax.optimization_barrier((gradient_held, own))
    above_held = lax.ppermute(gradient_here, "mem", down)
    below_held = lax.ppermute(gradient_here, "mem", up)
    other_held = lax.ppermute(gradient_here, "mem", swap)
    above_held, below_held, other_held, own_low, own_high = lax.optimization_barrier(
        (above_held, below_held, other_held, own_low, own_high)
    )
    near = jnp.stack([above_held, below_held, other_held])
    far = lax.ppermute(near, "mem", swap)

    sums = None
    groups = [(0, own, own_low, own_high)]
    for first, size, gradient, skip in (
        (2, 6, near, 0),
        (8, 3, far, 0),
        (11, 1, far, 3),
    ):
        start = jnp.full((1,), first, jnp.int32)
        turned, control = prepare(
            first, size, order, start, perturbations, gradient, skip, turned
        )
        low, upper = halos(control)
        groups.append((first, control, low, upper))
    for first, control, low, upper in groups:
        sums = collect(first, weights, low, control, upper, turned, sums)
    theirs, ours = sums
    kept = ours + lax.ppermute(theirs, "mem", swap)
    from_below = lax.ppermute(kept[:, 2:4].astype(jnp.bfloat16), "mem", up)
    from_above = lax.ppermute(kept[:, 4:6].astype(jnp.bfloat16), "mem", down)
    return kept[:, :2] + from_below.astype(jnp.float32) + from_above.astype(jnp.float32)


def solution(mesh):
    placed = (P("mem", None, None, "lat", None), P(None, "mem", "lat", None), P())
    return jax.shard_map(
        local, mesh=mesh, in_specs=placed, out_specs=P(None, "mem", "lat", None), check_vma=False
    )
```

```python
import functools
import math

import jax
import jax.numpy as jnp
from jax import lax
from jax.experimental import pallas as pl
from jax.experimental.pallas import tpu as pltpu
from jax.sharding import PartitionSpec as P

LANES = 128
VMEM_LIMIT = 24 * 1024 * 1024
WIDE_LIMIT = 57 * 1024 * 1024
COST = pl.CostEstimate(flops=1000, bytes_accessed=1000, transcendentals=0)


def weights_for(spread_cells):
    return [
        math.exp(-(offset * offset) / (2.0 * spread_cells * spread_cells))
        for offset in range(-4, 5)
    ]


LON_W = weights_for(3.0)
LEV_W = weights_for(2.0)
LAT_W = weights_for(2.5)


def turn_level(pert_ref, turned_ref):
    for slot in range(pert_ref.shape[1]):
        turned = jnp.transpose(pert_ref[:, slot, 0].astype(jnp.float32), (1, 0, 2))
        turned_ref[0, :, slot] = turned.astype(jnp.bfloat16)


def control_level(turned_ref, grad_ref, pair, level, packed_ref):
    slots, rows, lon = grad_ref.shape[1], grad_ref.shape[3], grad_ref.shape[4]
    full = lon // LANES
    tails = []
    for row in range(rows):
        for tile in range(full + 1):
            lanes = slice(tile * LANES, min((tile + 1) * LANES, lon))
            value = None
            for slot in range(slots):
                term = (
                    turned_ref[0, row, slot, :, lanes].astype(jnp.float32)
                    * grad_ref[pair, slot, level, row : row + 1, lanes]
                )
                value = term if value is None else value + term
            if tile < full:
                packed_ref[0, row * full + tile] = value.astype(jnp.bfloat16)
            else:
                tails.append(value)
    packed_ref[0, rows * full] = jnp.concatenate(tails, axis=1).astype(jnp.bfloat16)


def prepare_kernel(levels_ref, base_ref, pert_ref, grad_ref, turned_ref, packed_ref):
    turn_level(pert_ref, turned_ref)
    control_level(turned_ref, grad_ref, 0, pl.program_id(0), packed_ref)


def prepare(levels, base, perturbations, gradient):
    members, slots, count, rows, lon = perturbations.shape
    entries = rows * (lon // LANES) + 1
    return pl.pallas_call(
        prepare_kernel,
        out_shape=(
            jax.ShapeDtypeStruct((count, rows, slots, members, lon), jnp.bfloat16),
            jax.ShapeDtypeStruct((2, entries, members, LANES), jnp.bfloat16),
        ),
        grid_spec=pltpu.PrefetchScalarGridSpec(
            num_scalar_prefetch=2,
            grid=(2,),
            in_specs=[
                pl.BlockSpec(
                    (members, slots, 1, rows, lon), lambda i, lev, b: (0, 0, lev[b[0] + i], 0, 0)
                ),
                pl.BlockSpec(gradient.shape, lambda i, lev, b: (0, 0, 0, 0, 0)),
            ],
            out_specs=(
                pl.BlockSpec((1, rows, slots, members, lon), lambda i, lev, b: (i, 0, 0, 0, 0)),
                pl.BlockSpec((1, entries, members, LANES), lambda i, lev, b: (i, 0, 0, 0)),
            ),
        ),
        name="prepare",
        cost_estimate=COST,
        compiler_params=pltpu.CompilerParams(vmem_limit_bytes=WIDE_LIMIT),
    )(levels, base, perturbations, gradient)


def turn_kernel(levels_ref, pert_ref, turned_in_ref, turned_ref):
    turn_level(pert_ref, turned_ref)


def turn_rest(levels, perturbations, turned):
    members, slots, count, rows, lon = perturbations.shape
    return pl.pallas_call(
        turn_kernel,
        out_shape=jax.ShapeDtypeStruct(turned.shape, turned.dtype),
        grid_spec=pltpu.PrefetchScalarGridSpec(
            num_scalar_prefetch=1,
            grid=(count - 2,),
            in_specs=[
                pl.BlockSpec(
                    (members, slots, 1, rows, lon), lambda i, lev: (0, 0, lev[2 + i], 0, 0)
                ),
                pl.BlockSpec(memory_space=pl.ANY),
            ],
            out_specs=pl.BlockSpec(
                (1, rows, slots, members, lon), lambda i, lev: (2 + i, 0, 0, 0, 0)
            ),
        ),
        input_output_aliases={2: 0},
        name="turn",
        cost_estimate=COST,
        compiler_params=pltpu.CompilerParams(vmem_limit_bytes=WIDE_LIMIT),
    )(levels, perturbations, turned)


def control_kernel(turned_ref, *refs):
    packed_ref = refs[-1]
    step = pl.program_id(0)
    for pair, grad_ref in enumerate(refs[:-1]):

        @pl.when(step // 2 == pair)
        def _():
            control_level(turned_ref, grad_ref, 0, step % 2, packed_ref)


def control_of(first, turned, gradients):
    count, rows, slots, members, lon = turned.shape
    entries = rows * (lon // LANES) + 1
    size = 2 * len(gradients)
    return pl.pallas_call(
        control_kernel,
        out_shape=jax.ShapeDtypeStruct((size, entries, members, LANES), jnp.bfloat16),
        grid=(size,),
        in_specs=[
            pl.BlockSpec((1, rows, slots, members, lon), lambda i: (first + i, 0, 0, 0, 0))
        ]
        + [
            pl.BlockSpec((1,) + gradient.shape[1:], lambda i: (0, 0, 0, 0, 0))
            for gradient in gradients
        ],
        out_specs=pl.BlockSpec((1, entries, members, LANES), lambda i: (i, 0, 0, 0)),
        name="control",
        cost_estimate=COST,
        compiler_params=pltpu.CompilerParams(vmem_limit_bytes=56320 * 1024),
    )(turned, *gradients)


def smooth_level(refs, out_ref, level, wide_ref, rows, lon):
    full, rest = lon // LANES, lon % LANES
    members = refs[0].shape[2]
    for tile in range(full + 1):
        if tile < full:
            source = [
                ref[0, row * full + tile].astype(jnp.float32) for ref in refs for row in range(rows)
            ]
        else:
            tails = [ref[0, rows * full].astype(jnp.float32) for ref in refs]
            source = [
                tail if row == 0 else pltpu.roll(tail, LANES - row * rest, 1)
                for tail in tails
                for row in range(rows)
            ]
        for row in range(rows):
            total = LAT_W[4] * source[row + 4]
            for step in range(1, 5):
                total = total + LAT_W[4 + step] * (source[row + 4 - step] + source[row + 4 + step])
            wide_ref[row, :, tile * LANES : (tile + 1) * LANES] = total
    half = 8
    lane = lax.broadcasted_iota(jnp.int32, (half, LANES), 1)
    for row in range(rows):
        for part in range(members // half):
            some = slice(part * half, (part + 1) * half)
            tiles = [
                wide_ref[row, some, tile * LANES : (tile + 1) * LANES] for tile in range(full + 1)
            ]
            before = pltpu.roll(tiles[full], LANES - rest, 1)
            tiles[full] = jnp.where(lane < rest, tiles[full], pltpu.roll(tiles[0], rest, 1))
            tiles = [before] + tiles

            def moved(arrays, step):
                rolled = [pltpu.roll(array, -step % LANES, 1) for array in arrays]
                if step > 0:
                    return [
                        jnp.where(lane < LANES - step, here, after)
                        for here, after in zip(rolled, rolled[1:] + rolled[-1:])
                    ]
                return [
                    jnp.where(lane < -step, former, here)
                    for former, here in zip(rolled[:1] + rolled[:-1], rolled)
                ]

            last, following = moved(tiles, -1), moved(tiles, 1)
            inner = [LON_W[1] * tile for tile in tiles]
            lower = [
                LON_W[0] * a + b + LON_W[2] * c for a, b, c in zip(last, inner, following)
            ]
            upper = [
                LON_W[2] * a + b + LON_W[0] * c for a, b, c in zip(last, inner, following)
            ]
            lower, upper = moved(lower, -3), moved(upper, 3)
            for tile in range(full + 1):
                k = tile + 1
                total = LON_W[4] * tiles[k] + LON_W[3] * (last[k] + following[k])
                out_ref[level, row, some, tile * LANES : (tile + 1) * LANES] = (
                    total + lower[k] + upper[k]
                )


def sums_of(arrays, sub):
    for width in (1, 2, 4):
        low = (sub & width) == 0
        arrays = [
            jnp.where(low, even, odd) + pltpu.roll(jnp.where(low, odd, even), width, 0)
            for even, odd in zip(arrays[::2], arrays[1::2])
        ]
    return arrays[0]


def collect_pair(pair, first, fields_ref, weight_ref, pert_ref, before_ref, out_ref, lon):
    size, rows, members, _ = fields_ref.shape
    full = lon // LANES
    slots = out_ref.shape[0]
    weights = [
        [weight_ref[2 * pair + i, first + source] for source in range(size)]
        for i in range(2)
    ]
    for tile in range(full + 1):
        lanes = slice(tile * LANES, min((tile + 1) * LANES, lon))
        across = min((tile + 1) * LANES, lon) - tile * LANES
        sub = lax.broadcasted_iota(jnp.int32, (8, across), 0)
        products = [[[None] * rows for _ in range(slots)] for _ in range(2)]
        for row in range(rows):
            values = [fields_ref[source, row, :, lanes] for source in range(size)]
            for i in range(2):
                total = weights[i][0] * values[0]
                for source in range(1, size):
                    total = total + weights[i][source] * values[source]
                for slot in range(slots):
                    product = total * pert_ref[2 * pair + i, row, slot, :, lanes].astype(jnp.float32)
                    product = product.reshape(members // 8, 8, across)
                    part = product[0]
                    for other in range(1, members // 8):
                        part = part + product[other]
                    products[i][slot][row] = part
        for i in range(2):
            value = sums_of(products[i][0] + products[i][1], sub)
            for slot in range(slots):
                piece = value[slot * rows : (slot + 1) * rows]
                if before_ref is not None:
                    piece = piece + before_ref[slot, i, :, lanes]
                out_ref[slot, i, :, lanes] = piece


def collect_kernel(weight_ref, low_ref, own_ref, high_ref, pert_ref, *refs, first, lon):
    theirs_ref, ours_ref, fields_ref, wide_ref = refs[-4:]
    theirs_before, ours_before = refs[:2] if len(refs) > 4 else (None, None)
    size, rows = fields_ref.shape[:2]
    step = pl.program_id(0)
    half = (pl.num_programs(0) - size) // 2

    @pl.when(step < size)
    def _():
        smooth_level((low_ref, own_ref, high_ref), fields_ref, step, wide_ref, rows, lon)

    @pl.when((step >= size) & (step < size + half))
    def _():
        pair = step - size + half
        collect_pair(
            pair, first, fields_ref, weight_ref, pert_ref, theirs_before, theirs_ref, lon
        )

    @pl.when(step >= size + half)
    def _():
        pair = step - size - half
        collect_pair(pair, first, fields_ref, weight_ref, pert_ref, ours_before, ours_ref, lon)


def collect(first, weights, low, own, high, turned, before):
    count, rows, slots, members, lon = turned.shape
    size, entries = own.shape[:2]
    pairs = count // 2
    half = pairs // 2
    width = (lon // LANES + 1) * LANES
    level = pl.BlockSpec(
        (1, entries, members, LANES), lambda i, w: (jnp.minimum(i, size - 1), 0, 0, 0)
    )
    theirs = pl.BlockSpec(
        (slots, 2, rows, lon), lambda i, w: (0, jnp.clip(i - size, 0, half - 1), 0, 0)
    )
    ours = pl.BlockSpec(
        (slots, 2, rows, lon), lambda i, w: (0, jnp.clip(i - size - half, 0, half - 1), 0, 0)
    )
    pert = pl.BlockSpec(memory_space=pltpu.VMEM)
    result = jax.ShapeDtypeStruct((slots, count // 2, rows, lon), jnp.float32)
    return pl.pallas_call(
        functools.partial(collect_kernel, first=first, lon=lon),
        out_shape=(result, result),
        grid_spec=pltpu.PrefetchScalarGridSpec(
            num_scalar_prefetch=1,
            grid=(size + pairs,),
            in_specs=[level] * 3 + [pert] + ([] if before is None else [theirs, ours]),
            out_specs=(theirs, ours),
            scratch_shapes=[
                pltpu.VMEM((size, rows, members, width), jnp.float32),
                pltpu.VMEM((rows, members, width), jnp.float32),
            ],
        ),
        name="collect",
        cost_estimate=COST,
        compiler_params=pltpu.CompilerParams(vmem_limit_bytes=VMEM_LIMIT),
    )(weights, low, own, high, turned, *(() if before is None else before))


def local(perturbations, gradient_held, block_owner):
    members, slots, levels, rows, lon = perturbations.shape
    across = lax.axis_size("mem") // 2
    place = lax.axis_index("mem")
    high, core = place // 2, place % 2

    swap = [(2 * z + c, 2 * z + 1 - c) for z in range(across) for c in range(2)]
    down = [(2 * ((z + 1) % across) + c, 2 * z + c) for z in range(across) for c in range(2)]
    up = [(2 * z + c, 2 * ((z + 1) % across) + c) for z in range(across) for c in range(2)]
    count = lax.axis_size("lat")
    forward = [(i, i + 1) for i in range(count - 1)]
    backward = [(i + 1, i) for i in range(count - 1)]

    index = jnp.arange(levels, dtype=jnp.int32)
    pair = index // 2
    shift = jnp.where(pair % 3 == 0, 0, jnp.where(pair % 3 == 1, 1, across - 1))
    flip = jnp.where(pair >= 3, 1 - core, core)
    positions = 2 * (2 * ((high + shift) % across) + flip) + index % 2
    order = jnp.sum(
        jnp.where(
            positions[:, None] == index[None, :], block_owner.astype(jnp.int32)[None, :], 0
        ),
        axis=1,
    ).astype(jnp.int32)
    apart = jnp.abs(order[:, None] - order[None, :])
    weights = jnp.zeros((levels, levels), jnp.float32)
    for step in range(5):
        weights = jnp.where(apart == step, LEV_W[4 + step], weights)

    def halos(control):
        return lax.ppermute(control, "lat", forward), lax.ppermute(control, "lat", backward)

    base = (2 * place).astype(jnp.int32).reshape(1)
    turned, own = prepare(
        block_owner.astype(jnp.int32), base, perturbations, gradient_held[None]
    )
    own_low, own_high = halos(own)
    gradient_here, _ = lax.optimization_barrier((gradient_held, own))
    near = [
        lax.ppermute(gradient_here, "mem", down),
        lax.ppermute(gradient_here, "mem", up),
        lax.ppermute(gradient_here, "mem", swap),
    ]
    turned = turn_rest(order, perturbations, turned)
    *near, own_low, own_high = lax.optimization_barrier((*near, own_low, own_high))
    mid = control_of(2, turned, [gradient[None] for gradient in near])
    mid_low, mid_high = halos(mid)
    far = [lax.ppermute(gradient, "mem", swap) for gradient in near[:2]]
    last = control_of(8, turned, [gradient[None] for gradient in far])
    last_low, last_high = halos(last)

    sums = None
    groups = (
        (0, own, own_low, own_high),
        (2, mid, mid_low, mid_high),
        (8, last, last_low, last_high),
    )
    for first, control, low, upper in groups:
        sums = collect(first, weights, low, control, upper, turned, sums)
    theirs, ours = sums
    kept = ours + lax.ppermute(theirs, "mem", swap)
    from_below = lax.ppermute(kept[:, 2:4].astype(jnp.bfloat16), "mem", up)
    from_above = lax.ppermute(kept[:, 4:6].astype(jnp.bfloat16), "mem", down)
    return kept[:, :2] + from_below.astype(jnp.float32) + from_above.astype(jnp.float32)


def solution(mesh):
    placed = (P("mem", None, None, "lat", None), P(None, "mem", "lat", None), P())
    return jax.shard_map(
        local, mesh=mesh, in_specs=placed, out_specs=P(None, "mem", "lat", None), check_vma=False
    )
```

```python
import functools
import math

import jax
import jax.numpy as jnp
from jax import lax
from jax.experimental import pallas as pl
from jax.experimental.pallas import tpu as pltpu
from jax.sharding import PartitionSpec as P

LANES = 128
VMEM_LIMIT = 24 * 1024 * 1024
COST = pl.CostEstimate(flops=1000, bytes_accessed=1000, transcendentals=0)


def weights_for(spread_cells):
    return [
        math.exp(-(offset * offset) / (2.0 * spread_cells * spread_cells))
        for offset in range(-4, 5)
    ]


LON_W = weights_for(3.0)
LEV_W = weights_for(2.0)
LAT_W = weights_for(2.5)


def prepare_kernel(levels_ref, base_ref, pert_ref, grad_ref, *refs):
    turned_ref, packed_ref = refs[-2:]
    slots, rows, lon = grad_ref.shape[1], grad_ref.shape[3], grad_ref.shape[4]
    full = lon // LANES
    for slot in range(slots):
        turned = jnp.transpose(pert_ref[:, slot, 0].astype(jnp.float32), (1, 0, 2))
        turned_ref[0, :, slot] = turned.astype(jnp.bfloat16)
    tails = []
    for row in range(rows):
        for tile in range(full + 1):
            lanes = slice(tile * LANES, min((tile + 1) * LANES, lon))
            value = None
            for slot in range(slots):
                term = (
                    turned_ref[0, row, slot, :, lanes].astype(jnp.float32)
                    * grad_ref[0, slot, 0, row : row + 1, lanes]
                )
                value = term if value is None else value + term
            if tile < full:
                packed_ref[0, row * full + tile] = value.astype(jnp.bfloat16)
            else:
                tails.append(value)
    packed_ref[0, rows * full] = jnp.concatenate(tails, axis=1).astype(jnp.bfloat16)


def prepare(
    first, size, levels, base, perturbations, gradient, skip=0, turned=None, limit=VMEM_LIMIT
):
    members, slots, count, rows, lon = perturbations.shape
    entries = rows * (lon // LANES) + 1
    inputs = [perturbations, gradient]
    in_specs = [
        pl.BlockSpec(
            (members, slots, 1, rows, lon), lambda i, lev, b: (0, 0, lev[b[0] + i], 0, 0)
        ),
        pl.BlockSpec(
            (1, slots, 1, rows, lon),
            lambda i, lev, b: ((i + skip) // 2, 0, (i + skip) % 2, 0, 0),
        ),
    ]
    aliases = {}
    if turned is not None:
        inputs.append(turned)
        in_specs.append(pl.BlockSpec(memory_space=pl.ANY))
        aliases = {4: 0}
    return pl.pallas_call(
        prepare_kernel,
        out_shape=(
            jax.ShapeDtypeStruct((count, rows, slots, members, lon), jnp.bfloat16),
            jax.ShapeDtypeStruct((size, entries, members, LANES), jnp.bfloat16),
        ),
        grid_spec=pltpu.PrefetchScalarGridSpec(
            num_scalar_prefetch=2,
            grid=(size,),
            in_specs=in_specs,
            out_specs=(
                pl.BlockSpec(
                    (1, rows, slots, members, lon),
                    lambda i, lev, b: (first + i, 0, 0, 0, 0),
                ),
                pl.BlockSpec((1, entries, members, LANES), lambda i, lev, b: (i, 0, 0, 0)),
            ),
        ),
        input_output_aliases=aliases,
        name="prepare",
        cost_estimate=COST,
        compiler_params=pltpu.CompilerParams(vmem_limit_bytes=limit),
    )(levels, base, *inputs)


def smooth_level(refs, out_ref, level, wide_ref, rows, lon):
    full, rest = lon // LANES, lon % LANES
    members = refs[0].shape[2]
    for tile in range(full + 1):
        if tile < full:
            source = [
                ref[0, row * full + tile].astype(jnp.float32) for ref in refs for row in range(rows)
            ]
        else:
            tails = [ref[0, rows * full].astype(jnp.float32) for ref in refs]
            source = [
                tail if row == 0 else pltpu.roll(tail, LANES - row * rest, 1)
                for tail in tails
                for row in range(rows)
            ]
        for row in range(rows):
            total = LAT_W[4] * source[row + 4]
            for step in range(1, 5):
                total = total + LAT_W[4 + step] * (source[row + 4 - step] + source[row + 4 + step])
            wide_ref[row, :, tile * LANES : (tile + 1) * LANES] = total
    half = 8
    lane = lax.broadcasted_iota(jnp.int32, (half, LANES), 1)
    for row in range(rows):
        for part in range(members // half):
            some = slice(part * half, (part + 1) * half)
            tiles = [
                wide_ref[row, some, tile * LANES : (tile + 1) * LANES] for tile in range(full + 1)
            ]
            before = pltpu.roll(tiles[full], LANES - rest, 1)
            tiles[full] = jnp.where(lane < rest, tiles[full], pltpu.roll(tiles[0], rest, 1))
            tiles = [before] + tiles

            def moved(arrays, step):
                rolled = [pltpu.roll(array, -step % LANES, 1) for array in arrays]
                if step > 0:
                    return [
                        jnp.where(lane < LANES - step, here, after)
                        for here, after in zip(rolled, rolled[1:] + rolled[-1:])
                    ]
                return [
                    jnp.where(lane < -step, former, here)
                    for former, here in zip(rolled[:1] + rolled[:-1], rolled)
                ]

            last, following = moved(tiles, -1), moved(tiles, 1)
            inner = [LON_W[1] * tile for tile in tiles]
            lower = [
                LON_W[0] * a + b + LON_W[2] * c for a, b, c in zip(last, inner, following)
            ]
            upper = [
                LON_W[2] * a + b + LON_W[0] * c for a, b, c in zip(last, inner, following)
            ]
            lower, upper = moved(lower, -3), moved(upper, 3)
            for tile in range(full + 1):
                k = tile + 1
                total = LON_W[4] * tiles[k] + LON_W[3] * (last[k] + following[k])
                out_ref[level, row, some, tile * LANES : (tile + 1) * LANES] = (
                    total + lower[k] + upper[k]
                )


def sums_of(arrays, sub):
    for width in (1, 2, 4):
        low = (sub & width) == 0
        arrays = [
            jnp.where(low, even, odd) + pltpu.roll(jnp.where(low, odd, even), width, 0)
            for even, odd in zip(arrays[::2], arrays[1::2])
        ]
    return arrays[0]


def collect_pair(pair, first, fields_ref, weight_ref, pert_ref, before_ref, out_ref, lon):
    size, rows, members, _ = fields_ref.shape
    full = lon // LANES
    slots = out_ref.shape[0]
    weights = [
        [weight_ref[2 * pair + i, first + source] for source in range(size)]
        for i in range(2)
    ]
    for tile in range(full + 1):
        lanes = slice(tile * LANES, min((tile + 1) * LANES, lon))
        across = min((tile + 1) * LANES, lon) - tile * LANES
        sub = lax.broadcasted_iota(jnp.int32, (8, across), 0)
        products = [[[None] * rows for _ in range(slots)] for _ in range(2)]
        for row in range(rows):
            values = [fields_ref[source, row, :, lanes] for source in range(size)]
            for i in range(2):
                total = weights[i][0] * values[0]
                for source in range(1, size):
                    total = total + weights[i][source] * values[source]
                for slot in range(slots):
                    product = total * pert_ref[2 * pair + i, row, slot, :, lanes].astype(jnp.float32)
                    product = product.reshape(members // 8, 8, across)
                    part = product[0]
                    for other in range(1, members // 8):
                        part = part + product[other]
                    products[i][slot][row] = part
        for i in range(2):
            value = sums_of(products[i][0] + products[i][1], sub)
            for slot in range(slots):
                piece = value[slot * rows : (slot + 1) * rows]
                if before_ref is not None:
                    piece = piece + before_ref[slot, i, :, lanes]
                out_ref[slot, i, :, lanes] = piece


def collect_kernel(weight_ref, low_ref, own_ref, high_ref, pert_ref, *refs, first, lon):
    theirs_ref, ours_ref, fields_ref, wide_ref = refs[-4:]
    theirs_before, ours_before = refs[:2] if len(refs) > 4 else (None, None)
    size, rows = fields_ref.shape[:2]
    step = pl.program_id(0)
    half = (pl.num_programs(0) - size) // 2

    @pl.when(step < size)
    def _():
        smooth_level((low_ref, own_ref, high_ref), fields_ref, step, wide_ref, rows, lon)

    @pl.when((step >= size) & (step < size + half))
    def _():
        pair = step - size + half
        collect_pair(
            pair, first, fields_ref, weight_ref, pert_ref, theirs_before, theirs_ref, lon
        )

    @pl.when(step >= size + half)
    def _():
        pair = step - size - half
        collect_pair(pair, first, fields_ref, weight_ref, pert_ref, ours_before, ours_ref, lon)


def collect(first, weights, low, own, high, turned, before):
    count, rows, slots, members, lon = turned.shape
    size, entries = own.shape[:2]
    pairs = count // 2
    half = pairs // 2
    width = (lon // LANES + 1) * LANES
    level = pl.BlockSpec(
        (1, entries, members, LANES), lambda i, w: (jnp.minimum(i, size - 1), 0, 0, 0)
    )
    theirs = pl.BlockSpec(
        (slots, 2, rows, lon), lambda i, w: (0, jnp.clip(i - size, 0, half - 1), 0, 0)
    )
    ours = pl.BlockSpec(
        (slots, 2, rows, lon), lambda i, w: (0, jnp.clip(i - size - half, 0, half - 1), 0, 0)
    )
    pert = pl.BlockSpec(memory_space=pltpu.VMEM)
    result = jax.ShapeDtypeStruct((slots, count // 2, rows, lon), jnp.float32)
    return pl.pallas_call(
        functools.partial(collect_kernel, first=first, lon=lon),
        out_shape=(result, result),
        grid_spec=pltpu.PrefetchScalarGridSpec(
            num_scalar_prefetch=1,
            grid=(size + pairs,),
            in_specs=[level] * 3 + [pert] + ([] if before is None else [theirs, ours]),
            out_specs=(theirs, ours),
            scratch_shapes=[
                pltpu.VMEM((size, rows, members, width), jnp.float32),
                pltpu.VMEM((rows, members, width), jnp.float32),
            ],
        ),
        name="collect",
        cost_estimate=COST,
        compiler_params=pltpu.CompilerParams(vmem_limit_bytes=VMEM_LIMIT),
    )(weights, low, own, high, turned, *(() if before is None else before))


def first_kernel(weight_ref, low_ref, own_ref, high_ref, pert_ref, *refs, first, lon):
    before_ref, theirs_ref, fields_ref, wide_ref = refs
    size, rows = fields_ref.shape[:2]
    step = pl.program_id(0)

    @pl.when(step < size)
    def _():
        smooth_level((low_ref, own_ref, high_ref), fields_ref, step, wide_ref, rows, lon)

    @pl.when(step >= size)
    def _():
        pair = step - size + pl.num_programs(0) - size
        collect_pair(
            pair, first, fields_ref, weight_ref, pert_ref, before_ref, theirs_ref, lon
        )


def second_kernel(weight_ref, fields_ref, pert_ref, before_ref, ours_ref, *, first, lon):
    pair = pl.program_id(0)
    collect_pair(pair, first, fields_ref, weight_ref, pert_ref, before_ref, ours_ref, lon)


def collect_last(first, weights, low, own, high, turned, before):
    count, rows, slots, members, lon = turned.shape
    size, entries = own.shape[:2]
    half = count // 4
    width = (lon // LANES + 1) * LANES
    level = pl.BlockSpec(
        (1, entries, members, LANES), lambda i, w: (jnp.minimum(i, size - 1), 0, 0, 0)
    )
    moved = pl.BlockSpec((slots, 2, rows, lon), lambda i, w: (0, jnp.maximum(i - size, 0), 0, 0))
    still = pl.BlockSpec((slots, 2, rows, lon), lambda i, w: (0, i, 0, 0))
    resident = pl.BlockSpec(memory_space=pltpu.VMEM)
    result = jax.ShapeDtypeStruct((slots, count // 2, rows, lon), jnp.float32)
    theirs, fields = pl.pallas_call(
        functools.partial(first_kernel, first=first, lon=lon),
        out_shape=(
            result,
            jax.ShapeDtypeStruct((size, rows, members, width), jnp.float32),
        ),
        grid_spec=pltpu.PrefetchScalarGridSpec(
            num_scalar_prefetch=1,
            grid=(size + half,),
            in_specs=[level] * 3 + [resident, moved],
            out_specs=(moved, resident),
            scratch_shapes=[pltpu.VMEM((rows, members, width), jnp.float32)],
        ),
        name="collect_theirs",
        cost_estimate=COST,
        compiler_params=pltpu.CompilerParams(vmem_limit_bytes=VMEM_LIMIT),
    )(weights, low, own, high, turned, before[0])
    ours = pl.pallas_call(
        functools.partial(second_kernel, first=first, lon=lon),
        out_shape=result,
        grid_spec=pltpu.PrefetchScalarGridSpec(
            num_scalar_prefetch=1,
            grid=(half,),
            in_specs=[resident, resident, still],
            out_specs=still,
        ),
        name="collect_ours",
        cost_estimate=COST,
        compiler_params=pltpu.CompilerParams(vmem_limit_bytes=VMEM_LIMIT),
    )(weights, fields, turned, before[1])
    return theirs, ours


def local(perturbations, gradient_held, block_owner):
    members, slots, levels, rows, lon = perturbations.shape
    across = lax.axis_size("mem") // 2
    place = lax.axis_index("mem")
    high, core = place // 2, place % 2

    swap = [(2 * z + c, 2 * z + 1 - c) for z in range(across) for c in range(2)]
    down = [(2 * ((z + 1) % across) + c, 2 * z + c) for z in range(across) for c in range(2)]
    up = [(2 * z + c, 2 * ((z + 1) % across) + c) for z in range(across) for c in range(2)]
    count = lax.axis_size("lat")
    forward = [(i, i + 1) for i in range(count - 1)]
    backward = [(i + 1, i) for i in range(count - 1)]

    index = jnp.arange(levels, dtype=jnp.int32)
    pair = index // 2
    shift = jnp.where(pair % 3 == 0, 0, jnp.where(pair % 3 == 1, 1, across - 1))
    flip = jnp.where(pair >= 3, 1 - core, core)
    positions = 2 * (2 * ((high + shift) % across) + flip) + index % 2
    order = jnp.sum(
        jnp.where(
            positions[:, None] == index[None, :], block_owner.astype(jnp.int32)[None, :], 0
        ),
        axis=1,
    ).astype(jnp.int32)
    apart = jnp.abs(order[:, None] - order[None, :])
    weights = jnp.zeros((levels, levels), jnp.float32)
    for step in range(5):
        weights = jnp.where(apart == step, LEV_W[4 + step], weights)

    def halos(control, after=None):
        lower, upper = control, control
        if after is not None:
            lower, _ = lax.optimization_barrier((control, after[0]))
            upper, _ = lax.optimization_barrier((control, after[1]))
        return lax.ppermute(lower, "lat", forward), lax.ppermute(upper, "lat", backward)

    turned, own = prepare(
        0,
        2,
        block_owner.astype(jnp.int32),
        (2 * place).astype(jnp.int32).reshape(1),
        perturbations,
        gradient_held[None],
        limit=57 * 1024 * 1024,
    )
    own_low, own_high = halos(own)
    gradient_here, _ = lax.optimization_barrier((gradient_held, own))
    near = [
        lax.ppermute(gradient_here, "mem", down),
        lax.ppermute(gradient_here, "mem", up),
        lax.ppermute(gradient_here, "mem", swap),
    ]
    near = jnp.stack(near)
    far = lax.ppermute(near, "mem", swap)

    sums = None
    groups = [(0, own, own_low, own_high)]
    for first, size, gradient, skip in ((2, 6, near, 0), (8, 4, far, 0)):
        start = jnp.full((1,), first, jnp.int32)
        turned, control = prepare(
            first, size, order, start, perturbations, gradient, skip, turned
        )
        low, upper = halos(control, (own_low, own_high) if first == 2 else None)
        groups.append((first, control, low, upper))
    for first, control, low, upper in groups[:-1]:
        sums = collect(first, weights, low, control, upper, turned, sums)
    first, control, low, upper = groups[-1]
    theirs, ours = collect_last(first, weights, low, control, upper, turned, sums)
    kept = ours + lax.ppermute(theirs, "mem", swap)
    from_below = lax.ppermute(kept[:, 2:4].astype(jnp.bfloat16), "mem", up)
    from_above = lax.ppermute(kept[:, 4:6].astype(jnp.bfloat16), "mem", down)
    return kept[:, :2] + from_below.astype(jnp.float32) + from_above.astype(jnp.float32)


def solution(mesh):
    placed = (P("mem", None, None, "lat", None), P(None, "mem", "lat", None), P())
    return jax.shard_map(
        local, mesh=mesh, in_specs=placed, out_specs=P(None, "mem", "lat", None), check_vma=False
    )
```

```python
import functools
import math

import jax
import jax.numpy as jnp
from jax import lax
from jax.experimental import pallas as pl
from jax.experimental.pallas import tpu as pltpu
from jax.sharding import PartitionSpec as P

LANES = 128
VMEM_LIMIT = 24 * 1024 * 1024
COST = pl.CostEstimate(flops=1000, bytes_accessed=1000, transcendentals=0)


def weights_for(spread_cells):
    return [
        math.exp(-(offset * offset) / (2.0 * spread_cells * spread_cells))
        for offset in range(-4, 5)
    ]


LON_W = weights_for(3.0)
LEV_W = weights_for(2.0)
LAT_W = weights_for(2.5)


def prepare_kernel(levels_ref, base_ref, pert_ref, grad_ref, *refs):
    turned_ref, packed_ref = refs[-2:]
    slots, rows, lon = grad_ref.shape[1], grad_ref.shape[3], grad_ref.shape[4]
    full = lon // LANES
    for slot in range(slots):
        turned = jnp.transpose(pert_ref[:, slot, 0].astype(jnp.float32), (1, 0, 2))
        turned_ref[0, :, slot] = turned.astype(jnp.bfloat16)
    tails = []
    for row in range(rows):
        for tile in range(full + 1):
            lanes = slice(tile * LANES, min((tile + 1) * LANES, lon))
            value = None
            for slot in range(slots):
                term = (
                    turned_ref[0, row, slot, :, lanes].astype(jnp.float32)
                    * grad_ref[0, slot, 0, row : row + 1, lanes]
                )
                value = term if value is None else value + term
            if tile < full:
                packed_ref[0, row * full + tile] = value.astype(jnp.bfloat16)
            else:
                tails.append(value)
    packed_ref[0, rows * full] = jnp.concatenate(tails, axis=1).astype(jnp.bfloat16)


def prepare(
    first, size, levels, base, perturbations, gradient, skip=0, turned=None, limit=VMEM_LIMIT
):
    members, slots, count, rows, lon = perturbations.shape
    entries = rows * (lon // LANES) + 1
    inputs = [perturbations, gradient]
    in_specs = [
        pl.BlockSpec(
            (members, slots, 1, rows, lon), lambda i, lev, b: (0, 0, lev[b[0] + i], 0, 0)
        ),
        pl.BlockSpec(
            (1, slots, 1, rows, lon),
            lambda i, lev, b: ((i + skip) // 2, 0, (i + skip) % 2, 0, 0),
        ),
    ]
    aliases = {}
    if turned is not None:
        inputs.append(turned)
        in_specs.append(pl.BlockSpec(memory_space=pl.ANY))
        aliases = {4: 0}
    return pl.pallas_call(
        prepare_kernel,
        out_shape=(
            jax.ShapeDtypeStruct((count, rows, slots, members, lon), jnp.bfloat16),
            jax.ShapeDtypeStruct((size, entries, members, LANES), jnp.bfloat16),
        ),
        grid_spec=pltpu.PrefetchScalarGridSpec(
            num_scalar_prefetch=2,
            grid=(size,),
            in_specs=in_specs,
            out_specs=(
                pl.BlockSpec(
                    (1, rows, slots, members, lon),
                    lambda i, lev, b: (first + i, 0, 0, 0, 0),
                ),
                pl.BlockSpec((1, entries, members, LANES), lambda i, lev, b: (i, 0, 0, 0)),
            ),
        ),
        input_output_aliases=aliases,
        name="prepare",
        cost_estimate=COST,
        compiler_params=pltpu.CompilerParams(vmem_limit_bytes=limit),
    )(levels, base, *inputs)


def smooth_level(refs, out_ref, level, wide_ref, rows, lon):
    full, rest = lon // LANES, lon % LANES
    members = refs[0].shape[2]
    for tile in range(full + 1):
        if tile < full:
            source = [
                ref[0, row * full + tile].astype(jnp.float32) for ref in refs for row in range(rows)
            ]
        else:
            tails = [ref[0, rows * full].astype(jnp.float32) for ref in refs]
            source = [
                tail if row == 0 else pltpu.roll(tail, LANES - row * rest, 1)
                for tail in tails
                for row in range(rows)
            ]
        for row in range(rows):
            total = LAT_W[4] * source[row + 4]
            for step in range(1, 5):
                total = total + LAT_W[4 + step] * (source[row + 4 - step] + source[row + 4 + step])
            wide_ref[row, :, tile * LANES : (tile + 1) * LANES] = total
    half = 8
    lane = lax.broadcasted_iota(jnp.int32, (half, LANES), 1)
    for row in range(rows):
        for part in range(members // half):
            some = slice(part * half, (part + 1) * half)
            tiles = [
                wide_ref[row, some, tile * LANES : (tile + 1) * LANES] for tile in range(full + 1)
            ]
            before = pltpu.roll(tiles[full], LANES - rest, 1)
            tiles[full] = jnp.where(lane < rest, tiles[full], pltpu.roll(tiles[0], rest, 1))
            tiles = [before] + tiles

            def moved(arrays, step):
                rolled = [pltpu.roll(array, -step % LANES, 1) for array in arrays]
                if step > 0:
                    return [
                        jnp.where(lane < LANES - step, here, after)
                        for here, after in zip(rolled, rolled[1:] + rolled[-1:])
                    ]
                return [
                    jnp.where(lane < -step, former, here)
                    for former, here in zip(rolled[:1] + rolled[:-1], rolled)
                ]

            last, following = moved(tiles, -1), moved(tiles, 1)
            inner = [LON_W[1] * tile for tile in tiles]
            lower = [
                LON_W[0] * a + b + LON_W[2] * c for a, b, c in zip(last, inner, following)
            ]
            upper = [
                LON_W[2] * a + b + LON_W[0] * c for a, b, c in zip(last, inner, following)
            ]
            lower, upper = moved(lower, -3), moved(upper, 3)
            for tile in range(full + 1):
                k = tile + 1
                total = LON_W[4] * tiles[k] + LON_W[3] * (last[k] + following[k])
                out_ref[level, row, some, tile * LANES : (tile + 1) * LANES] = (
                    total + lower[k] + upper[k]
                )


def sums_of(arrays, sub):
    for width in (1, 2, 4):
        low = (sub & width) == 0
        arrays = [
            jnp.where(low, even, odd) + pltpu.roll(jnp.where(low, odd, even), width, 0)
            for even, odd in zip(arrays[::2], arrays[1::2])
        ]
    return arrays[0]


def collect_pair(pair, first, fields_ref, weight_ref, pert_ref, before_ref, out_ref, lon):
    size, rows, members, _ = fields_ref.shape
    full = lon // LANES
    slots = out_ref.shape[0]
    weights = [
        [weight_ref[2 * pair + i, first + source] for source in range(size)]
        for i in range(2)
    ]
    for tile in range(full + 1):
        lanes = slice(tile * LANES, min((tile + 1) * LANES, lon))
        across = min((tile + 1) * LANES, lon) - tile * LANES
        sub = lax.broadcasted_iota(jnp.int32, (8, across), 0)
        products = [[[None] * rows for _ in range(slots)] for _ in range(2)]
        for row in range(rows):
            values = [fields_ref[source, row, :, lanes] for source in range(size)]
            for i in range(2):
                total = weights[i][0] * values[0]
                for source in range(1, size):
                    total = total + weights[i][source] * values[source]
                for slot in range(slots):
                    product = total * pert_ref[2 * pair + i, row, slot, :, lanes].astype(jnp.float32)
                    product = product.reshape(members // 8, 8, across)
                    part = product[0]
                    for other in range(1, members // 8):
                        part = part + product[other]
                    products[i][slot][row] = part
        for i in range(2):
            value = sums_of(products[i][0] + products[i][1], sub)
            for slot in range(slots):
                piece = value[slot * rows : (slot + 1) * rows]
                if before_ref is not None:
                    piece = piece + before_ref[slot, i, :, lanes]
                out_ref[slot, i, :, lanes] = piece


def collect_kernel(weight_ref, low_ref, own_ref, high_ref, pert_ref, *refs, first, lon):
    theirs_ref, ours_ref, fields_ref, wide_ref = refs[-4:]
    theirs_before, ours_before = refs[:2] if len(refs) > 4 else (None, None)
    size, rows = fields_ref.shape[:2]
    step = pl.program_id(0)
    half = (pl.num_programs(0) - size) // 2

    @pl.when(step < size)
    def _():
        smooth_level((low_ref, own_ref, high_ref), fields_ref, step, wide_ref, rows, lon)

    @pl.when((step >= size) & (step < size + half))
    def _():
        pair = step - size + half
        collect_pair(
            pair, first, fields_ref, weight_ref, pert_ref, theirs_before, theirs_ref, lon
        )

    @pl.when(step >= size + half)
    def _():
        pair = step - size - half
        collect_pair(pair, first, fields_ref, weight_ref, pert_ref, ours_before, ours_ref, lon)


def collect(first, weights, low, own, high, turned, before):
    count, rows, slots, members, lon = turned.shape
    size, entries = own.shape[:2]
    pairs = count // 2
    half = pairs // 2
    width = (lon // LANES + 1) * LANES
    level = pl.BlockSpec(
        (1, entries, members, LANES), lambda i, w: (jnp.minimum(i, size - 1), 0, 0, 0)
    )
    theirs = pl.BlockSpec(
        (slots, 2, rows, lon), lambda i, w: (0, jnp.clip(i - size, 0, half - 1), 0, 0)
    )
    ours = pl.BlockSpec(
        (slots, 2, rows, lon), lambda i, w: (0, jnp.clip(i - size - half, 0, half - 1), 0, 0)
    )
    pert = pl.BlockSpec(memory_space=pltpu.VMEM)
    result = jax.ShapeDtypeStruct((slots, count // 2, rows, lon), jnp.float32)
    return pl.pallas_call(
        functools.partial(collect_kernel, first=first, lon=lon),
        out_shape=(result, result),
        grid_spec=pltpu.PrefetchScalarGridSpec(
            num_scalar_prefetch=1,
            grid=(size + pairs,),
            in_specs=[level] * 3 + [pert] + ([] if before is None else [theirs, ours]),
            out_specs=(theirs, ours),
            scratch_shapes=[
                pltpu.VMEM((size, rows, members, width), jnp.float32),
                pltpu.VMEM((rows, members, width), jnp.float32),
            ],
        ),
        name="collect",
        cost_estimate=COST,
        compiler_params=pltpu.CompilerParams(vmem_limit_bytes=VMEM_LIMIT),
    )(weights, low, own, high, turned, *(() if before is None else before))


def first_kernel(weight_ref, low_ref, own_ref, high_ref, pert_ref, *refs, first, lon):
    before_ref, theirs_ref, fields_ref, wide_ref = refs
    size, rows = fields_ref.shape[:2]
    step = pl.program_id(0)

    @pl.when(step < size)
    def _():
        smooth_level((low_ref, own_ref, high_ref), fields_ref, step, wide_ref, rows, lon)

    @pl.when(step >= size)
    def _():
        pair = step - size + pl.num_programs(0) - size
        collect_pair(
            pair, first, fields_ref, weight_ref, pert_ref, before_ref, theirs_ref, lon
        )


def second_kernel(weight_ref, fields_ref, pert_ref, before_ref, ours_ref, *, first, lon):
    pair = pl.program_id(0)
    collect_pair(pair, first, fields_ref, weight_ref, pert_ref, before_ref, ours_ref, lon)


def collect_last(first, weights, low, own, high, turned, before):
    count, rows, slots, members, lon = turned.shape
    size, entries = own.shape[:2]
    half = count // 4
    width = (lon // LANES + 1) * LANES
    level = pl.BlockSpec(
        (1, entries, members, LANES), lambda i, w: (jnp.minimum(i, size - 1), 0, 0, 0)
    )
    moved = pl.BlockSpec((slots, 2, rows, lon), lambda i, w: (0, jnp.maximum(i - size, 0), 0, 0))
    still = pl.BlockSpec((slots, 2, rows, lon), lambda i, w: (0, i, 0, 0))
    resident = pl.BlockSpec(memory_space=pltpu.VMEM)
    result = jax.ShapeDtypeStruct((slots, count // 2, rows, lon), jnp.float32)
    theirs, fields = pl.pallas_call(
        functools.partial(first_kernel, first=first, lon=lon),
        out_shape=(
            result,
            jax.ShapeDtypeStruct((size, rows, members, width), jnp.float32),
        ),
        grid_spec=pltpu.PrefetchScalarGridSpec(
            num_scalar_prefetch=1,
            grid=(size + half,),
            in_specs=[level] * 3 + [resident, moved],
            out_specs=(moved, resident),
            scratch_shapes=[pltpu.VMEM((rows, members, width), jnp.float32)],
        ),
        name="collect_theirs",
        cost_estimate=COST,
        compiler_params=pltpu.CompilerParams(vmem_limit_bytes=VMEM_LIMIT),
    )(weights, low, own, high, turned, before[0])
    ours = pl.pallas_call(
        functools.partial(second_kernel, first=first, lon=lon),
        out_shape=result,
        grid_spec=pltpu.PrefetchScalarGridSpec(
            num_scalar_prefetch=1,
            grid=(half,),
            in_specs=[resident, resident, still],
            out_specs=still,
        ),
        name="collect_ours",
        cost_estimate=COST,
        compiler_params=pltpu.CompilerParams(vmem_limit_bytes=VMEM_LIMIT),
    )(weights, fields, turned, before[1])
    return theirs, ours


def local(perturbations, gradient_held, block_owner):
    members, slots, levels, rows, lon = perturbations.shape
    across = lax.axis_size("mem") // 2
    place = lax.axis_index("mem")
    high, core = place // 2, place % 2

    swap = [(2 * z + c, 2 * z + 1 - c) for z in range(across) for c in range(2)]
    down = [(2 * ((z + 1) % across) + c, 2 * z + c) for z in range(across) for c in range(2)]
    up = [(2 * z + c, 2 * ((z + 1) % across) + c) for z in range(across) for c in range(2)]
    count = lax.axis_size("lat")
    forward = [(i, i + 1) for i in range(count - 1)]
    backward = [(i + 1, i) for i in range(count - 1)]

    index = jnp.arange(levels, dtype=jnp.int32)
    pair = index // 2
    shift = jnp.where(pair % 3 == 0, 0, jnp.where(pair % 3 == 1, 1, across - 1))
    flip = jnp.where(pair >= 3, 1 - core, core)
    positions = 2 * (2 * ((high + shift) % across) + flip) + index % 2
    order = jnp.sum(
        jnp.where(
            positions[:, None] == index[None, :], block_owner.astype(jnp.int32)[None, :], 0
        ),
        axis=1,
    ).astype(jnp.int32)
    apart = jnp.abs(order[:, None] - order[None, :])
    weights = jnp.zeros((levels, levels), jnp.float32)
    for step in range(5):
        weights = jnp.where(apart == step, LEV_W[4 + step], weights)

    def halos(control, after=None):
        lower, upper = control, control
        if after is not None:
            lower = lax.optimization_barrier((control, after[0], *after[2:]))[0]
            upper = lax.optimization_barrier((control, after[1], *after[2:]))[0]
        return lax.ppermute(lower, "lat", forward), lax.ppermute(upper, "lat", backward)

    turned, own = prepare(
        0,
        2,
        block_owner.astype(jnp.int32),
        (2 * place).astype(jnp.int32).reshape(1),
        perturbations,
        gradient_held[None],
        limit=57 * 1024 * 1024,
    )
    own_low, own_high = halos(own)
    gradient_here, _ = lax.optimization_barrier((gradient_held, own))
    near = [
        lax.ppermute(gradient_here, "mem", down),
        lax.ppermute(gradient_here, "mem", up),
        lax.ppermute(gradient_here, "mem", swap),
    ]
    near = jnp.stack(near)
    far = lax.ppermute(near, "mem", swap)

    sums = None
    groups = [(0, own, own_low, own_high)]
    for first, size, gradient, skip in ((2, 6, near, 0), (8, 2, far, 0), (10, 2, far, 2)):
        start = jnp.full((1,), first, jnp.int32)
        turned, control = prepare(
            first, size, order, start, perturbations, gradient, skip, turned
        )
        after = groups[0][2:] if first == 2 else None
        if first == 10:
            sums = collect(0, weights, own_low, own, own_high, turned, None)
            after = (*groups[1][2:], sums[0])
        low, upper = halos(control, after)
        groups.append((first, control, low, upper))
    for first, control, low, upper in groups[1:-1]:
        sums = collect(first, weights, low, control, upper, turned, sums)
    first, control, low, upper = groups[-1]
    theirs, ours = collect_last(first, weights, low, control, upper, turned, sums)
    kept = ours + lax.ppermute(theirs, "mem", swap)
    from_below = lax.ppermute(kept[:, 2:4].astype(jnp.bfloat16), "mem", up)
    from_above = lax.ppermute(kept[:, 4:6].astype(jnp.bfloat16), "mem", down)
    return kept[:, :2] + from_below.astype(jnp.float32) + from_above.astype(jnp.float32)


def solution(mesh):
    placed = (P("mem", None, None, "lat", None), P(None, "mem", "lat", None), P())
    return jax.shard_map(
        local, mesh=mesh, in_specs=placed, out_specs=P(None, "mem", "lat", None), check_vma=False
    )
```
